32 devices in a mesh: gx: 8 (over z, y), gy: 4 (over x, core).
Axes of the slice: x: 2, y: 2, z: 4, core: 2. Of those that a mesh axis runs over, the one named last changes fastest.
Arguments:
- layer_in: bfloat16 [8192, 2048], P('gx', 'gy'), may hold values from -15 to 15
- attn_gain: float32 [2048], replicated, may hold values from 0.25 to 1.75
- q_gain: float32 [128], replicated, may hold values from 0.5 to 5
- k_gain: float32 [128], replicated, may hold values from 0.5 to 5
- w_query: bfloat16 [2048, 2048], P('gx', 'gy'), may hold values from -0.125 to 0.125
- w_key: bfloat16 [2048, 1024], P('gx', 'gy'), may hold values from -0.125 to 0.125
- w_value: bfloat16 [2048, 1024], P('gx', 'gy'), may hold values from -0.125 to 0.125
- w_output: bfloat16 [2048, 2048], P('gy', 'gx'), may hold values from -0.375 to 0.375
- mlp_gain: float32 [2048], replicated, may hold values from 0.25 to 1.75
- w_gate: bfloat16 [2048, 6144], P('gx', 'gy'), may hold values from -0.125 to 0.125
- w_up: bfloat16 [2048, 6144], P('gx', 'gy'), may hold values from -0.125 to 0.125
- w_down: bfloat16 [6144, 2048], P('gy', 'gx'), may hold values from -0.078125 to 0.078125
- out_grad: bfloat16 [8192, 2048], P('gx', 'gy'), may hold values from -6 to 6
Outputs:
- layer_out: bfloat16 [8192, 2048], P('gx', 'gy')
- input_grad: float32 [8192, 2048], P('gx', 'gy')
- attn_gain_grad: float32 [2048], replicated
- q_gain_grad: float32 [128], replicated
- k_gain_grad: float32 [128], replicated
- query_grad: float32 [2048, 2048], P('gx', 'gy')
- key_grad: float32 [2048, 1024], P('gx', 'gy')
- value_grad: float32 [2048, 1024], P('gx', 'gy')
- output_grad: float32 [2048, 2048], P('gy', 'gx')
- mlp_gain_grad: float32 [2048], replicated
- gate_grad: float32 [2048, 6144], P('gx', 'gy')
- up_grad: float32 [2048, 6144], P('gx', 'gy')
- down_grad: float32 [6144, 2048], P('gy', 'gx')
The draws below stay inside these ranges and needn't reach their ends.
All inputs are finite; a program needn't handle non-finite values.
Results may differ from the reference program's by a relative error of at most 0.02.
The reference program's roundings to bfloat16 on the way count: a program that leaves them out, or rounds other values in their place, can miss the bound.
Values may be sent and summed in bfloat16 or wider, within the bound.
No kernel may reach another device: no remote copies, remote signals or barrier semaphores. Data moves between devices by JAX's collectives and lax.ppermute only.
A program may use at most 256 MiB of HBM per device.

```python
import math
import jax
import jax.numpy as jnp
from jax import lax

D = 2048
HQ = 16
HK = 8
HD = 128
FF = 6144
L = 512
TOKENS = 8192


def draw_layer_in(key, part):
    sub_key = jax.random.fold_in(key, 303)
    position = jnp.arange(D, dtype=jnp.float32) / (D - 1.0)
    entries = jnp.clip(jax.random.normal(sub_key, (TOKENS, D), jnp.float32), -6.0, 6.0)
    feature_scale = jnp.exp(jnp.log(0.4) + position * jnp.log(6.25))
    return (entries * feature_scale[None, :]).astype(jnp.bfloat16)


def draw_q_gain(key, part):
    sub_key = jax.random.fold_in(key, 101)
    return jax.random.uniform(sub_key, (HD,), jnp.float32, 0.5, 2.0)


def draw_k_gain(key, part):
    sub_key = jax.random.fold_in(key, 202)
    return jax.random.uniform(sub_key, (HD,), jnp.float32, 0.5, 2.0)


def block_levels(key, dims, pieces, least, top_value):
    loudness = 1.0
    for dim, blocks in pieces:
        draws = jax.random.uniform(jax.random.fold_in(jax.random.fold_in(key, 6), dim), (blocks,), jnp.float32, least / len(pieces), top_value / len(pieces))
        loudness = loudness * jnp.repeat(jnp.exp(draws), dims[dim] // blocks).reshape((-1,) + (1,) * (len(dims) - 1 - dim))
    return loudness


def scatter_about(own_key, dims, spread, bound, pieces=(), kind=jnp.bfloat16):
    drawn = jax.random.normal(own_key, dims, jnp.float32) * spread
    if len(pieces) > 0:
        drawn = block_levels(own_key, dims, pieces, -0.22, 0.18) * drawn
    return jnp.clip(drawn, min=-bound, max=bound).astype(kind)


def setup_inputs(seed: int = 0) -> dict:
    key_of = jax.random.split(jax.random.key(seed), 14)
    return {
        "layer_in": draw_layer_in(jax.random.fold_in(key_of[13], 71), 0),
        "attn_gain": jnp.clip(1.0 + 0.15 * jax.random.normal(key_of[1], (D,), jnp.float32), 0.25, 1.75),
        "q_gain": draw_q_gain(jax.random.fold_in(key_of[13], 71), 0),
        "k_gain": draw_k_gain(jax.random.fold_in(key_of[13], 71), 0),
        "w_query": scatter_about(key_of[4], (D, HQ * HD), D ** -0.5, 0.125, ((0, 8), (1, 4))),
        "w_key": scatter_about(key_of[5], (D, HK * HD), D ** -0.5, 0.125, ((0, 8), (1, 4))),
        "w_value": scatter_about(key_of[6], (D, HK * HD), D ** -0.5, 0.125, ((0, 8), (1, 4))),
        "w_output": scatter_about(key_of[7], (HQ * HD, D), (HQ * HD // 8) ** -0.5, 0.375, ((0, 4), (1, 8))),
        "mlp_gain": jnp.clip(1.0 + 0.15 * jax.random.normal(key_of[8], (D,), jnp.float32), 0.25, 1.75),
        "w_gate": scatter_about(key_of[9], (D, FF), D ** -0.5, 0.125, ((0, 8), (1, 4))),
        "w_up": scatter_about(key_of[10], (D, FF), D ** -0.5, 0.125, ((0, 8), (1, 4))),
        "w_down": scatter_about(key_of[11], (FF, D), FF ** -0.5, 0.078125, ((0, 4), (1, 8))),
        "out_grad": scatter_about(key_of[12], (TOKENS, D), 1.0, 6.0, ((0, 8), (1, 4))),
    }


epsilon = 1e-06
rope_base = 1000000.0

def rope_tables(length, dim_width):
    half_width = dim_width // 2
    frequency = rope_base ** (-(jnp.arange(half_width, dtype=jnp.float32) * (2.0 / dim_width)))
    angles = jnp.arange(length, dtype=jnp.float32)[:, None] * frequency[None, :]
    angles = jnp.concatenate([angles, angles], axis=1)
    return (jnp.cos(angles), jnp.sin(angles))

def rotate(tensor):
    half_width = tensor.shape[-1] // 2
    return jnp.concatenate([-tensor[..., half_width:], tensor[..., :half_width]], axis=-1)

def rotate_back(tensor):
    half_width = tensor.shape[-1] // 2
    return jnp.concatenate([tensor[..., half_width:], -tensor[..., :half_width]], axis=-1)

def head_norm(tensor, gain_vec):
    factor = lax.rsqrt(lax.optimization_barrier(jnp.mean(tensor * tensor, axis=-1, keepdims=True)) + epsilon)
    return (tensor * factor * gain_vec, factor)

def head_norm_back(upstream, tensor, factor, gain_vec):
    weighted = upstream * gain_vec
    return factor * weighted - tensor * factor ** 3 * lax.optimization_barrier(jnp.mean(weighted * tensor, axis=-1, keepdims=True))

def matmul(left, right):
    return jnp.dot(left, right, preferred_element_type=jnp.float32)

def fein(form, left, right):
    return jnp.einsum(form, left.astype(jnp.float32), right.astype(jnp.float32))

def causal_scores(query_rot, key_rot):
    inv_scale = 1.0 / math.sqrt(HD)
    scores = fein('sihgc,sjhc->shgij', query_rot, key_rot) * inv_scale
    causal = jnp.arange(L)[:, None] >= jnp.arange(L)[None, :]
    return jnp.where(causal, scores, -1e+30)

def block_pass(layer_in, out_grad, attn_gain, q_gain, k_gain, w_query, w_key, w_value, w_output, mlp_gain, w_gate, w_up, w_down):
    row_count = layer_in.shape[0]
    seq_count = row_count // L
    group_size = HQ // HK
    inv_scale = 1.0 / math.sqrt(HD)
    in_float = layer_in.astype(jnp.float32)
    scale_one = lax.rsqrt(lax.optimization_barrier(jnp.mean(in_float * in_float, axis=1, keepdims=True)) + epsilon)
    normed_one = (in_float * scale_one * attn_gain).astype(jnp.bfloat16)
    query_act = matmul(normed_one, w_query).reshape(row_count, HQ, HD)
    key_act = matmul(normed_one, w_key).reshape(row_count, HK, HD)
    values = matmul(normed_one, w_value).astype(jnp.bfloat16).reshape(seq_count, L, HK, HD)
    query_normed, query_factor = head_norm(query_act, q_gain)
    key_normed, key_factor = head_norm(key_act, k_gain)
    cosine, sine = rope_tables(L, HD)
    cosine = cosine[None, :, None, :]
    sine = sine[None, :, None, :]
    query_seq = query_normed.reshape(seq_count, L, HQ, HD)
    key_seq = key_normed.reshape(seq_count, L, HK, HD)
    query_rot = (query_seq * cosine + rotate(query_seq) * sine).astype(jnp.bfloat16).reshape(seq_count, L, HK, group_size, HD)
    key_rot = (key_seq * cosine + rotate(key_seq) * sine).astype(jnp.bfloat16)
    scores = causal_scores(query_rot, key_rot)
    row_top = lax.optimization_barrier(jnp.max(scores, axis=-1, keepdims=True))
    log_total = row_top + jnp.log(lax.optimization_barrier(jnp.sum(jnp.exp(scores - row_top), axis=-1, keepdims=True)))
    probs = jnp.exp(scores - log_total).astype(jnp.bfloat16)
    attended = fein('shgij,sjhc->sihgc', probs, values).astype(jnp.bfloat16)
    attended_flat = attended.reshape(row_count, HQ * HD)
    mid_float = in_float + matmul(attended_flat, w_output)
    scale_two = lax.rsqrt(lax.optimization_barrier(jnp.mean(mid_float * mid_float, axis=1, keepdims=True)) + epsilon)
    normed_two = (mid_float * scale_two * mlp_gain).astype(jnp.bfloat16)
    gate_act = matmul(normed_two, w_gate)
    up_act = matmul(normed_two, w_up)
    sigmoid_gate = jax.nn.sigmoid(gate_act)
    hidden = (gate_act * sigmoid_gate * up_act).astype(jnp.bfloat16)
    layer_out = (mid_float + matmul(hidden, w_down)).astype(jnp.bfloat16)
    grad_float = out_grad.astype(jnp.float32)
    grad_hidden = matmul(out_grad, w_down.T)
    down_term = matmul(hidden.T, out_grad)
    grad_gate = (grad_hidden * up_act * sigmoid_gate * (1.0 + gate_act * (1.0 - sigmoid_gate))).astype(jnp.bfloat16)
    grad_up = (grad_hidden * gate_act * sigmoid_gate).astype(jnp.bfloat16)
    gate_term = matmul(normed_two.T, grad_gate)
    up_term = matmul(normed_two.T, grad_up)
    grad_two = matmul(grad_gate, w_gate.T) + matmul(grad_up, w_up.T)
    mlp_gain_term = lax.optimization_barrier(jnp.sum(grad_two * mid_float * scale_two, axis=0))
    grad_mid = grad_float + scale_two * mlp_gain * grad_two - mid_float * scale_two ** 3 * lax.optimization_barrier(jnp.mean(mlp_gain * grad_two * mid_float, axis=1, keepdims=True))
    grad_mid_bf = grad_mid.astype(jnp.bfloat16)
    grad_att = matmul(grad_mid_bf, w_output.T).astype(jnp.bfloat16)
    output_term = matmul(attended_flat.T, grad_mid_bf)
    grad_att_seq = grad_att.reshape(seq_count, L, HK, group_size, HD)
    probs_again = jnp.exp(causal_scores(query_rot, key_rot) - log_total)
    probs_bf = probs_again.astype(jnp.bfloat16)
    delta = fein('sihgc,sihgc->shgi', grad_att_seq, attended)
    grad_probs = fein('sihgc,sjhc->shgij', grad_att_seq, values)
    grad_scores = (probs_again * (grad_probs - delta[..., None])).astype(jnp.bfloat16)
    grad_qrot = (fein('shgij,sjhc->sihgc', grad_scores, key_rot) * inv_scale).reshape(seq_count, L, HQ, HD)
    grad_krot = fein('shgij,sihgc->sjhc', grad_scores, query_rot) * inv_scale
    grad_value_act = fein('shgij,sihgc->sjhc', probs_bf, grad_att_seq)
    grad_qn = (grad_qrot * cosine + rotate_back(grad_qrot * sine)).reshape(row_count, HQ, HD)
    grad_kn = (grad_krot * cosine + rotate_back(grad_krot * sine)).reshape(row_count, HK, HD)
    q_gain_term = lax.optimization_barrier(jnp.sum(grad_qn * query_act * query_factor, axis=(0, 1)))
    k_gain_term = lax.optimization_barrier(jnp.sum(grad_kn * key_act * key_factor, axis=(0, 1)))
    grad_query = head_norm_back(grad_qn, query_act, query_factor, q_gain).astype(jnp.bfloat16).reshape(row_count, HQ * HD)
    grad_key = head_norm_back(grad_kn, key_act, key_factor, k_gain).astype(jnp.bfloat16).reshape(row_count, HK * HD)
    grad_value = grad_value_act.astype(jnp.bfloat16).reshape(row_count, HK * HD)
    query_term = matmul(normed_one.T, grad_query)
    key_term = matmul(normed_one.T, grad_key)
    value_term = matmul(normed_one.T, grad_value)
    grad_one = matmul(grad_query, w_query.T) + matmul(grad_key, w_key.T) + matmul(grad_value, w_value.T)
    attn_gain_term = lax.optimization_barrier(jnp.sum(grad_one * in_float * scale_one, axis=0))
    input_grad = grad_mid + scale_one * attn_gain * grad_one - in_float * scale_one ** 3 * lax.optimization_barrier(jnp.mean(attn_gain * grad_one * in_float, axis=1, keepdims=True))
    terms = (attn_gain_term, q_gain_term, k_gain_term, query_term, key_term, value_term, output_term, mlp_gain_term, gate_term, up_term, down_term)
    return (layer_out, input_grad, terms)

def reference(layer_in, attn_gain, q_gain, k_gain, w_query, w_key, w_value, w_output, mlp_gain, w_gate, w_up, w_down, out_grad):
    seqs_all = TOKENS // L
    per_block = 8 if seqs_all % 8 == 0 else 1
    block_count = seqs_all // per_block
    block_rows = per_block * L
    inputs = layer_in.reshape(block_count, block_rows, D)
    cotangents = out_grad.reshape(block_count, block_rows, D)
    initial = (jnp.zeros((D,), jnp.float32), jnp.zeros((HD,), jnp.float32), jnp.zeros((HD,), jnp.float32), jnp.zeros((D, HQ * HD), jnp.float32), jnp.zeros((D, HK * HD), jnp.float32), jnp.zeros((D, HK * HD), jnp.float32), jnp.zeros((HQ * HD, D), jnp.float32), jnp.zeros((D,), jnp.float32), jnp.zeros((D, FF), jnp.float32), jnp.zeros((D, FF), jnp.float32), jnp.zeros((FF, D), jnp.float32))

    def advance(running, block_pair):
        block_out, block_grad, terms = block_pass(block_pair[0], block_pair[1], attn_gain, q_gain, k_gain, w_query, w_key, w_value, w_output, mlp_gain, w_gate, w_up, w_down)
        return (tuple((held + term for held, term in zip(running, terms))), (block_out, block_grad))
    totals, (outs_all, grads_all) = lax.scan(advance, initial, (inputs, cotangents))
    return (outs_all.reshape(TOKENS, D), grads_all.reshape(TOKENS, D), totals[0], totals[1], totals[2], totals[3], totals[4], totals[5], totals[6], totals[7], totals[8], totals[9], totals[10])
```

```python
import math

import jax
import jax.numpy as jnp
from jax import lax
from jax.sharding import Mesh, PartitionSpec as P

D = 2048
HQ = 16
HK = 8
HD = 128
L = 512
GROUP = HQ // HK

epsilon = 1e-06
rope_base = 1000000.0
BF = jnp.bfloat16
F32 = jnp.float32


def rope_tables(length, dim_width):
    half_width = dim_width // 2
    frequency = rope_base ** (-(jnp.arange(half_width, dtype=F32) * (2.0 / dim_width)))
    angles = jnp.arange(length, dtype=F32)[:, None] * frequency[None, :]
    angles = jnp.concatenate([angles, angles], axis=1)
    return (jnp.cos(angles), jnp.sin(angles))


def rotate(tensor):
    half_width = tensor.shape[-1] // 2
    return jnp.concatenate([-tensor[..., half_width:], tensor[..., :half_width]], axis=-1)


def rotate_back(tensor):
    half_width = tensor.shape[-1] // 2
    return jnp.concatenate([tensor[..., half_width:], -tensor[..., :half_width]], axis=-1)


def head_norm(tensor, gain_vec):
    factor = lax.rsqrt(jnp.mean(tensor * tensor, axis=-1, keepdims=True) + epsilon)
    return (tensor * factor * gain_vec, factor)


def head_norm_back(upstream, tensor, factor, gain_vec):
    weighted = upstream * gain_vec
    return factor * weighted - tensor * factor**3 * jnp.mean(
        weighted * tensor, axis=-1, keepdims=True
    )


def matmul(left, right):
    return jnp.dot(left, right, preferred_element_type=F32)


def matmul_nt(left, right):
    return lax.dot_general(left, right, (((1,), (1,)), ((), ())), preferred_element_type=F32)


def matmul_tn(left, right):
    return lax.dot_general(left, right, (((0,), (0,)), ((), ())), preferred_element_type=F32)


def bein(form, left, right):
    return jnp.einsum(form, left, right, preferred_element_type=F32)


def causal_scores(query_rot, key_rot):
    inv_scale = 1.0 / math.sqrt(HD)
    scores = bein("sihgc,sjhc->shgij", query_rot, key_rot) * inv_scale
    causal = jnp.arange(L)[:, None] >= jnp.arange(L)[None, :]
    return jnp.where(causal, scores, -1e30)


def swap(tensor, axis):
    return lax.ppermute(tensor, axis, [(0, 1), (1, 0)])


def half_of(tensor, which, axis):
    size = tensor.shape[axis] // 2
    return lax.dynamic_slice_in_dim(tensor, which * size, size, axis)


def merge(first, mine, theirs, axis):
    low = jnp.where(first, mine, theirs)
    high = jnp.where(first, theirs, mine)
    return jnp.concatenate([low, high], axis=axis)


def place(x, c, pieces):
    own, over_c, over_x, over_xc = pieces
    width = own.shape[1]
    out = jnp.zeros((own.shape[0], 4 * width), own.dtype)
    for piece, xb, cb in (
        (own, x, c),
        (over_c, x, 1 - c),
        (over_x, 1 - x, c),
        (over_xc, 1 - x, 1 - c),
    ):
        out = lax.dynamic_update_slice(out, piece, (0, (xb * 2 + cb) * width))
    return out


def relative(x, c, tensor, axis):
    width = tensor.shape[axis] // 4
    blocks = [
        lax.dynamic_slice_in_dim(tensor, (xb * 2 + cb) * width, width, axis)
        for xb, cb in ((1 - x, 1 - c), (x, 1 - c), (1 - x, c), (x, c))
    ]
    return jnp.concatenate(blocks, axis=axis)


def gather_tokens(own):
    half = own.shape[0] // 2
    over_x = swap(own, "x")
    over_y = swap(own, "y")
    over_c = swap(own, "c")
    diag_a = swap(over_x[:half], "y")
    diag_b = swap(over_y[half:], "x")
    over_xc = swap(over_x, "c")
    over_yc = swap(over_y, "c")
    diag_ac = swap(diag_a, "c")
    diag_bc = swap(diag_b, "c")
    diag = jnp.concatenate([diag_a, diag_b], axis=0)
    diag_c = jnp.concatenate([diag_ac, diag_bc], axis=0)
    return (own, over_c, over_x, over_xc), (over_y, over_yc, diag, diag_c)


def scatter_tokens(part, own, other):
    other_recv = swap(part(other, 0).astype(BF), "c")
    other_kept = part(other, 1) + other_recv.astype(F32)
    own_recv = swap(part(own, 0).astype(BF), "c")
    own_kept = part(own, 1) + own_recv.astype(F32)
    rows, width = own_kept.shape[0], own_kept.shape[1] // 2
    half = rows // 2
    far = other_kept[:, :width].astype(BF)
    by_y = swap(far[:half], "y").astype(F32)
    by_x = swap(far[half:], "x").astype(F32)
    to_x = own_kept[:, :width]
    to_x = jnp.concatenate([to_x[:half] + by_y, to_x[half:]], axis=0).astype(BF)
    to_y = other_kept[:, width:]
    to_y = jnp.concatenate([to_y[:half], to_y[half:] + by_x], axis=0).astype(BF)
    return own_kept[:, width:] + swap(to_x, "x").astype(F32) + swap(to_y, "y").astype(F32)


def sum_pair(tensor, axes):
    for axis in axes:
        tensor = tensor + swap(tensor, axis)
    return tensor


def sum_all(tensor, z_size):
    tensor = sum_pair(tensor, ("c", "x", "y"))
    step = 1
    while step < z_size:
        tensor = tensor + lax.ppermute(tensor, "z", [(i, i ^ step) for i in range(z_size)])
        step *= 2
    return tensor


def attention(qkv, q_gain, k_gain, cosine, sine):
    rows = qkv.shape[0]
    seqs = rows // L
    q_width = GROUP * HD
    query_act = qkv[:, :q_width].reshape(rows, GROUP, HD)
    key_act = qkv[:, q_width : q_width + HD].reshape(rows, 1, HD)
    values = qkv[:, q_width + HD :].astype(BF).reshape(seqs, L, 1, HD)
    query_normed, query_factor = head_norm(query_act, q_gain)
    key_normed, key_factor = head_norm(key_act, k_gain)
    query_seq = query_normed.reshape(seqs, L, GROUP, HD)
    key_seq = key_normed.reshape(seqs, L, 1, HD)
    query_rot = (
        (query_seq * cosine + rotate(query_seq) * sine).astype(BF).reshape(seqs, L, 1, GROUP, HD)
    )
    key_rot = (key_seq * cosine + rotate(key_seq) * sine).astype(BF)
    scores = causal_scores(query_rot, key_rot)
    row_top = jnp.max(scores, axis=-1, keepdims=True)
    log_total = row_top + jnp.log(jnp.sum(jnp.exp(scores - row_top), axis=-1, keepdims=True))
    probs = jnp.exp(scores - log_total).astype(BF)
    attended = bein("shgij,sjhc->sihgc", probs, values).astype(BF)
    saved = (query_act, query_factor, key_act, key_factor, query_rot, key_rot, values, log_total, attended)
    return attended.reshape(rows, q_width), saved


def attention_back(grad_att, saved, q_gain, k_gain, cosine, sine):
    query_act, query_factor, key_act, key_factor, query_rot, key_rot, values, log_total, attended = saved
    rows = grad_att.shape[0]
    seqs = rows // L
    inv_scale = 1.0 / math.sqrt(HD)
    grad_att_seq = grad_att.reshape(seqs, L, 1, GROUP, HD)
    probs_again = jnp.exp(causal_scores(query_rot, key_rot) - log_total)
    probs_bf = probs_again.astype(BF)
    delta = bein("sihgc,sihgc->shgi", grad_att_seq, attended)
    grad_probs = bein("sihgc,sjhc->shgij", grad_att_seq, values)
    grad_scores = (probs_again * (grad_probs - delta[..., None])).astype(BF)
    grad_qrot = (bein("shgij,sjhc->sihgc", grad_scores, key_rot) * inv_scale).reshape(
        seqs, L, GROUP, HD
    )
    grad_krot = bein("shgij,sihgc->sjhc", grad_scores, query_rot) * inv_scale
    grad_value_act = bein("shgij,sihgc->sjhc", probs_bf, grad_att_seq)
    grad_qn = (grad_qrot * cosine + rotate_back(grad_qrot * sine)).reshape(rows, GROUP, HD)
    grad_kn = (grad_krot * cosine + rotate_back(grad_krot * sine)).reshape(rows, 1, HD)
    q_part = jnp.sum(grad_qn * query_act * query_factor, axis=(0, 1))
    k_part = jnp.sum(grad_kn * key_act * key_factor, axis=(0, 1))
    grad_query = head_norm_back(grad_qn, query_act, query_factor, q_gain).reshape(rows, GROUP * HD)
    grad_key = head_norm_back(grad_kn, key_act, key_factor, k_gain).reshape(rows, HD)
    grad_value = grad_value_act.reshape(rows, HD)
    return (
        jnp.concatenate([grad_query, grad_key, grad_value], axis=1).astype(BF),
        q_part,
        k_part,
    )


def row_scale(rows):
    rows = rows.astype(F32)
    return lax.rsqrt(jnp.mean(rows * rows, axis=1, keepdims=True) + epsilon)


def make(z_size):
    def on_device(
        layer_in,
        attn_gain,
        q_gain,
        k_gain,
        w_query,
        w_key,
        w_value,
        w_output,
        mlp_gain,
        w_gate,
        w_up,
        w_down,
        out_grad,
    ):
        z, y, x, c = (lax.axis_index(name) for name in ("z", "y", "x", "c"))
        first = y == 0
        rows, part_width = layer_in.shape
        column = (x * 2 + c) * part_width

        def take(axis, *parts):
            mine = jnp.concatenate([half_of(w, y, 1 - axis) for w in parts], axis=1)
            theirs = jnp.concatenate([half_of(w, 1 - y, 1 - axis) for w in parts], axis=1)
            merged = merge(first, mine, swap(theirs, "y"), axis)
            return lax.all_gather(merged, "z", axis=axis, tiled=True)

        w_qkv = take(0, w_query, w_key, w_value)
        in_own, in_other = gather_tokens(layer_in)
        w_out = take(1, w_output)
        w_gate_f = take(0, w_gate)
        w_up_f = take(0, w_up)
        w_down_f = take(1, w_down)
        g_own, g_other = gather_tokens(out_grad)

        def normed(rows_full, gain):
            scale = row_scale(rows_full)
            return (rows_full.astype(F32) * scale * gain).astype(BF), scale

        n1_own, scale_one = normed(place(x, c, in_own), attn_gain)
        n1_other, _ = normed(place(x, c, in_other), attn_gain)
        cosine, sine = rope_tables(L, HD)
        cosine = cosine[None, :, None, :]
        sine = sine[None, :, None, :]
        att_own, saved_own = attention(matmul(n1_own, w_qkv), q_gain, k_gain, cosine, sine)
        att_other, saved_other = attention(matmul(n1_other, w_qkv), q_gain, k_gain, cosine, sine)

        w_out_r = relative(x, c, w_out, 1)
        side = lambda w, s: lax.slice_in_dim(w, s * (w.shape[1] // 2), (s + 1) * (w.shape[1] // 2), axis=1)
        side0 = lambda w, s: lax.slice_in_dim(w, s * (w.shape[0] // 2), (s + 1) * (w.shape[0] // 2), axis=0)
        attn_share = scatter_tokens(lambda a, s: matmul(a, side(w_out_r, s)), att_own, att_other)
        in_share = layer_in.astype(F32)
        mid_share = in_share + attn_share

        mid_own, mid_other = gather_tokens(mid_share.astype(BF))
        n2_own, scale_two = normed(place(x, c, mid_own), mlp_gain)
        n2_other, _ = normed(place(x, c, mid_other), mlp_gain)
        gf_own = place(x, c, g_own)
        gf_other = place(x, c, g_other)

        def ffn(n2):
            gate_act = matmul(n2, w_gate_f)
            up_act = matmul(n2, w_up_f)
            sig = jax.nn.sigmoid(gate_act)
            hidden = (gate_act * sig * up_act).astype(BF)
            return gate_act, up_act, hidden

        ffn_own = ffn(n2_own)
        ffn_other = ffn(n2_other)

        def to_share_rows(term):
            got = lax.psum_scatter(term.astype(BF), "z", scatter_dimension=0, tiled=True)
            mine = half_of(got, y, 0)
            return merge(first, mine, swap(half_of(got, 1 - y, 0), "y"), 1).astype(F32)

        def to_share_cols(term):
            got = lax.psum_scatter(term.astype(BF), "z", scatter_dimension=1, tiled=True)
            mine = half_of(got, y, 1)
            return merge(first, mine, swap(half_of(got, 1 - y, 1), "y"), 0).astype(F32)

        down_grad = to_share_cols(matmul_tn(ffn_own[2], gf_own) + matmul_tn(ffn_other[2], gf_other))

        def ffn_back(acts, g):
            gate_act, up_act, _ = acts
            sig = jax.nn.sigmoid(gate_act)
            grad_hidden = matmul_nt(g, w_down_f)
            grad_gate = (grad_hidden * up_act * sig * (1.0 + gate_act * (1.0 - sig))).astype(BF)
            grad_up = (grad_hidden * gate_act * sig).astype(BF)
            return grad_gate, grad_up

        gb_own = ffn_back(ffn_own, gf_own)
        gb_other = ffn_back(ffn_other, gf_other)
        gate_grad = to_share_rows(matmul_tn(n2_own, gb_own[0]) + matmul_tn(n2_other, gb_other[0]))
        up_grad = to_share_rows(matmul_tn(n2_own, gb_own[1]) + matmul_tn(n2_other, gb_other[1]))
        w_gate_r = relative(x, c, w_gate_f, 0)
        w_up_r = relative(x, c, w_up_f, 0)
        grad_two = scatter_tokens(
            lambda a, s: matmul_nt(a[0], side0(w_gate_r, s)) + matmul_nt(a[1], side0(w_up_r, s)),
            gb_own,
            gb_other,
        )
        w_down_r = relative(x, c, w_down_f, 1)
        mlp_share = scatter_tokens(
            lambda a, s: matmul(a, side(w_down_r, s)), ffn_own[2], ffn_other[2]
        )
        layer_out = (mid_share + mlp_share).astype(BF)

        mlp_gain_share = lax.dynamic_slice_in_dim(mlp_gain, column, part_width, 0)
        attn_gain_share = lax.dynamic_slice_in_dim(attn_gain, column, part_width, 0)
        stat_two = sum_pair(jnp.sum(mlp_gain_share * grad_two * mid_share, axis=1), ("c", "x"))
        grad_mid = (
            out_grad.astype(F32)
            + scale_two * mlp_gain_share * grad_two
            - mid_share * scale_two**3 * (stat_two / D)[:, None]
        )
        mlp_gain_own = jnp.sum(grad_two * mid_share * scale_two, axis=0)
        gm_own, gm_other = gather_tokens(grad_mid.astype(BF))
        gm_own = place(x, c, gm_own)
        gm_other = place(x, c, gm_other)
        output_grad = to_share_cols(matmul_tn(att_own, gm_own) + matmul_tn(att_other, gm_other))
        back_own, q_own, k_own = attention_back(
            matmul_nt(gm_own, w_out).astype(BF), saved_own, q_gain, k_gain, cosine, sine
        )
        back_other, q_other, k_other = attention_back(
            matmul_nt(gm_other, w_out).astype(BF), saved_other, q_gain, k_gain, cosine, sine
        )
        qkv_got = lax.psum_scatter(
            (matmul_tn(n1_own, back_own) + matmul_tn(n1_other, back_other)).astype(BF),
            "z",
            scatter_dimension=0,
            tiled=True,
        )
        qkv_mine = half_of(qkv_got, y, 0)
        qkv_theirs = swap(half_of(qkv_got, 1 - y, 0), "y")
        q_width = GROUP * HD
        cut = lambda lo, hi: merge(first, qkv_mine[:, lo:hi], qkv_theirs[:, lo:hi], 1).astype(F32)
        query_grad = cut(0, q_width)
        key_grad = cut(q_width, q_width + HD)
        value_grad = cut(q_width + HD, q_width + 2 * HD)
        w_qkv_r = relative(x, c, w_qkv, 0)
        grad_one = scatter_tokens(
            lambda a, s: matmul_nt(a, side0(w_qkv_r, s)), back_own, back_other
        )
        stat_one = sum_pair(jnp.sum(attn_gain_share * grad_one * in_share, axis=1), ("c", "x"))
        input_grad = (
            grad_mid
            + scale_one * attn_gain_share * grad_one
            - in_share * scale_one**3 * (stat_one / D)[:, None]
        )
        attn_gain_own = jnp.sum(grad_one * in_share * scale_one, axis=0)
        embed = lambda share: lax.dynamic_update_slice(jnp.zeros((D,), F32), share, (column,))
        sums = sum_all(
            jnp.concatenate([embed(attn_gain_own), embed(mlp_gain_own), q_own + q_other, k_own + k_other]),
            z_size,
        )
        return (
            layer_out,
            input_grad,
            sums[:D],
            sums[2 * D : 2 * D + HD],
            sums[2 * D + HD :],
            query_grad,
            key_grad,
            value_grad,
            output_grad,
            sums[D : 2 * D],
            gate_grad,
            up_grad,
            down_grad,
        )

    return on_device


def solution(mesh):
    gx, gy = mesh.shape["gx"], mesh.shape["gy"]
    y_size = HK // gy
    z_size = gx // y_size
    cube = Mesh(mesh.devices.reshape(z_size, y_size, gy // 2, 2), ("z", "y", "x", "c"))
    rows_cols = P(("z", "y"), ("x", "c"))
    cols_rows = P(("x", "c"), ("z", "y"))
    return jax.shard_map(
        make(z_size),
        mesh=cube,
        in_specs=(
            rows_cols,
            P(),
            P(),
            P(),
            rows_cols,
            rows_cols,
            rows_cols,
            cols_rows,
            P(),
            rows_cols,
            rows_cols,
            cols_rows,
            rows_cols,
        ),
        out_specs=(
            rows_cols,
            rows_cols,
            P(),
            P(),
            P(),
            rows_cols,
            rows_cols,
            rows_cols,
            cols_rows,
            P(),
            rows_cols,
            rows_cols,
            cols_rows,
        ),
        check_vma=False,
    )
```
